32 devices in a mesh: context: 4 (over x, core), tensor: 4 (over z), dp: 2 (over y).
Axes of the slice: x: 2, y: 2, z: 4, core: 2. Of those that a mesh axis runs over, the one named last changes fastest.
Arguments:
- queries: bfloat16 [1024, 64, 128], P(('dp', 'context'), 'tensor'), parts along dimension 0, may hold values from -160 to 160
- key_heads: bfloat16 [1024, 4, 128], P(('dp', 'context'), 'tensor'), parts along dimension 0, may hold values from -6 to 6
- value_heads: bfloat16 [1024, 4, 128], P(('dp', 'context'), 'tensor'), parts along dimension 0, may hold values from -6 to 6
- out_grad: bfloat16 [1024, 64, 128], P(('dp', 'context'), 'tensor'), parts along dimension 0, may hold values from -6 to 6
- layout: int32 [1024], P('dp'), parts along dimension 0, may hold values from 0 to 511, as said below
- documents: int32 [1024], P('dp'), parts along dimension 0, may hold values from 0 to 3, never falling along the last dimension, each value on 1 to 384 neighbouring positions
Outputs:
- output: bfloat16 [1024, 64, 128], P(('dp', 'context'), 'tensor'), parts along dimension 0
- query_grad: bfloat16 [1024, 64, 128], P(('dp', 'context'), 'tensor'), parts along dimension 0
- key_grad: float32 [1024, 512], P(('dp', 'context'), 'tensor'), parts along dimension 0
- value_grad: float32 [1024, 512], P(('dp', 'context'), 'tensor'), parts along dimension 0
The draws below stay inside these ranges and needn't reach their ends.
There are 2 independent parts, one for each index of `dp`. The reference program is written for one: setup_inputs(seed, part) draws one part's arguments, and reference() takes and returns one part's arrays. A program takes and returns all parts, laid end to end along the dimension named above; each array names one. Nothing has to cross between parts.
Inputs may be any that keep to these rules, and one draw needn't show every extreme that they name: `layout`: a permutation of the tokens made of aligned runs of 64 consecutive tokens; every device's rows are two such runs, in an order drawn from the seed.
All inputs are finite; a program needn't handle non-finite values.
Results may differ from the reference program's by a relative error of at most 0.0064.
Values may be sent and summed in bfloat16 or wider, within the bound.
A program may use at most 128 MiB of HBM per device.

```python
import math
import jax
import jax.numpy as jnp
import numpy as np
from jax import lax

HD = 128
GROUP = 16
KV_GROUPS = 4
TOK_DEV = 128
H = 64
SEQ = 512
DOCS = 4
DOC_MOST = 384
N_CONTEXT = 4


def paired_draw(key):
    key_seed = jax.random.fold_in(key, 101)
    query_seed = jax.random.fold_in(key, 202)
    key_vals = jnp.clip(jax.random.normal(key_seed, (SEQ, KV_GROUPS, HD), jnp.float32), -6.0, 6.0)
    query_vals = jnp.clip(jax.random.normal(query_seed, (SEQ, H, HD), jnp.float32), -6.0, 6.0)
    return (query_vals, key_vals)


def draw_queries(key, part):
    return paired_draw(key)[0].astype(jnp.bfloat16)


def draw_key_heads(key, part):
    return paired_draw(key)[1].astype(jnp.bfloat16)


def draw_layout(key, part):
    half_run = TOK_DEV // 2
    runs = jax.random.permutation(key, 2 * N_CONTEXT)
    return (runs[:, None] * half_run + jnp.arange(half_run, dtype=jnp.int32)[None, :]).reshape(-1).astype(jnp.int32)


def level_of(own_key, shape, cuts, low, high):
    def one(axis_at, shards_of):
        steps = jax.random.uniform(jax.random.fold_in(jax.random.fold_in(own_key, 6), axis_at), (shards_of,), jnp.float32, low / len(cuts), high / len(cuts))
        return jnp.repeat(jnp.exp(steps), shape[axis_at] // shards_of).reshape((-1,) + (1,) * (len(shape) - axis_at - 1))

    factor_of = one(*cuts[0])
    for cut in cuts[1:]:
        factor_of = factor_of * one(*cut)
    return factor_of


def length_profile(amount, total, bound, skew):
    weights = [(1 << 20) // math.isqrt(standing ** skew) + 1 for standing in range(2, amount + 1)]
    spare, given = total - bound - (amount - 1), [1] * (amount - 1)
    while spare > 0:
        free = [i for i in range(amount - 1) if given[i] < bound]
        pool, budget = sum([weights[i] for i in free]), spare
        for i in free:
            more = min(bound - given[i], max(1, budget * weights[i] // pool), spare)
            given[i] = given[i] + more
            spare = spare - more
    return np.array([bound] + given)


def ragged_sizes(key, count, total, limit, lean):
    if count == 2:
        one = jax.random.randint(key, (), max(1, total - limit), min(limit, total - 1) + 1)
        return jnp.stack([one, total - one])
    tallies = jnp.asarray(length_profile(count, total, limit, lean), jnp.int32)
    pairs = (count - 1) // 2
    donor, sink = tallies[1:1 + 2 * pairs:2], tallies[2:2 + 2 * pairs:2]
    margin = jnp.minimum(donor - 1, limit - sink)
    passed = jax.random.randint(jax.random.fold_in(key, 1), (pairs,), 0, 1 << 20) % (margin + 1)
    tallies = tallies.at[1:1 + 2 * pairs:2].set(donor - passed).at[2:2 + 2 * pairs:2].set(sink + passed)
    return tallies[jax.random.permutation(jax.random.fold_in(key, 2), count)]


def gaussian(stream_key, shape, scale, bound, cuts=(), kind=jnp.bfloat16):
    drawn = jax.random.normal(stream_key, shape, jnp.float32) * scale
    if len(cuts) > 0:
        drawn = level_of(stream_key, shape, cuts, -0.22, 0.18) * drawn
    return jnp.clip(drawn, min=-bound, max=bound).astype(kind)


def setup_inputs(seed: int = 0, part: int = 0) -> dict:
    streams_of = jax.random.split(jax.random.key(seed), 7)
    part_keys = jax.random.split(jax.random.fold_in(streams_of[6], part), 7)
    return {
        "queries": draw_queries(jax.random.fold_in(jax.random.fold_in(streams_of[6], part), 71), part),
        "key_heads": draw_key_heads(jax.random.fold_in(jax.random.fold_in(streams_of[6], part), 71), part),
        "value_heads": gaussian(part_keys[2], (SEQ, KV_GROUPS, HD), 1.0, 6.0, ((0, 4), (1, 4))),
        "out_grad": gaussian(part_keys[3], (SEQ, H, HD), 1.0, 6.0, ((0, 4), (1, 4))),
        "layout": draw_layout(jax.random.fold_in(jax.random.fold_in(streams_of[6], part), 71), part),
        "documents": jnp.searchsorted(jnp.cumsum(ragged_sizes(part_keys[5], DOCS, SEQ, DOC_MOST, 2)), jnp.arange(SEQ), side="right").astype(jnp.int32),
    }


THETA = 8000000.0

def rotary(source, places, direction):
    half_dim = source.shape[-1] // 2
    frequency = jnp.exp(-(2.0 * jnp.arange(half_dim, dtype=jnp.float32) / source.shape[-1]) * math.log(THETA))
    angles = places.astype(jnp.float32)[:, None] * frequency[None, :]
    cosine = jnp.cos(angles)[:, None, :]
    sine_part = direction * jnp.sin(angles)[:, None, :]
    first_half = source[..., :half_dim]
    second = source[..., half_dim:]
    return jnp.concatenate([first_half * cosine - second * sine_part, second * cosine + first_half * sine_part], axis=-1)

def doc_positions(documents):
    length = documents.shape[0]
    indices = jnp.arange(length, dtype=jnp.int32)
    starts_here = jnp.concatenate([jnp.ones((1,), dtype=bool), documents[1:] != documents[:-1]])
    firsts = lax.cummax(jnp.where(starts_here, indices, jnp.zeros_like(indices)), axis=0)
    return indices - firsts

def reference(queries, key_heads, value_heads, out_grad, layout, documents):
    positions = doc_positions(documents)
    places = jnp.take(positions, layout)
    doc_rows = jnp.take(documents, layout)
    scaling = 1.0 / math.sqrt(HD)
    query_rot = rotary(queries.astype(jnp.float32), places, 1.0).astype(jnp.bfloat16)
    key_rot = rotary(key_heads.astype(jnp.float32), places, 1.0).astype(jnp.bfloat16)
    allowed = (doc_rows[:, None] == doc_rows[None, :]) & (layout[None, :] <= layout[:, None])
    owners = np.arange(H) // GROUP
    query_heads = jnp.transpose(query_rot, (1, 0, 2))
    key_per_head = jnp.transpose(key_rot, (1, 0, 2))[owners]
    value_per_head = jnp.transpose(value_heads, (1, 0, 2))[owners]
    grad_heads = jnp.transpose(out_grad, (1, 0, 2))

    def one_head(operands):
        query_one, key_one, value_one, grad_one = operands
        scores = jnp.dot(query_one, key_one.T, preferred_element_type=jnp.float32) * scaling
        scores = jnp.where(allowed, scores, -1e+30)
        largest = lax.optimization_barrier(jnp.max(scores, axis=1, keepdims=True))
        weights = jnp.exp(scores - largest)
        attention = weights / lax.optimization_barrier(jnp.sum(weights, axis=1, keepdims=True))
        attention_b = attention.astype(jnp.bfloat16)
        result = jnp.dot(attention_b, value_one, preferred_element_type=jnp.float32).astype(jnp.bfloat16)
        dprobs = jnp.dot(grad_one, value_one.T, preferred_element_type=jnp.float32)
        row_delta = lax.optimization_barrier(jnp.sum(grad_one.astype(jnp.float32) * result.astype(jnp.float32), axis=1, keepdims=True))
        dscores = (attention * (dprobs - row_delta) * scaling).astype(jnp.bfloat16)
        return (result, jnp.dot(dscores, key_one, preferred_element_type=jnp.float32), jnp.dot(dscores.T, query_one, preferred_element_type=jnp.float32), jnp.dot(attention_b.T, grad_one, preferred_element_type=jnp.float32))
    results, query_rot_grad, key_rot_grad, value_terms = lax.map(one_head, (query_heads, key_per_head, value_per_head, grad_heads))
    output = jnp.transpose(results, (1, 0, 2))
    query_grad = rotary(jnp.transpose(query_rot_grad, (1, 0, 2)), places, -1.0).astype(jnp.bfloat16)
    key_sum = jnp.transpose(key_rot_grad.reshape(KV_GROUPS, GROUP, SEQ, HD).sum(axis=1), (1, 0, 2))
    key_grad = rotary(key_sum, places, -1.0).reshape(SEQ, KV_GROUPS * HD)
    value_grad = jnp.transpose(value_terms.reshape(KV_GROUPS, GROUP, SEQ, HD).sum(axis=1), (1, 0, 2)).reshape(SEQ, KV_GROUPS * HD)
    return (output, query_grad, key_grad, value_grad)
```

```python
import functools
import math

import jax
import jax.numpy as jnp
from jax import lax
from jax.experimental import pallas as pl
from jax.experimental.pallas import tpu as pltpu
from jax.sharding import PartitionSpec as P

THETA = 8000000.0
RUN = 64
MASKED = -1e30
MESH = pl.DeviceIdType.MESH
F32 = jnp.float32
BF16 = jnp.bfloat16


def dot(lhs, rhs, rhs_dim=0):
    return lax.dot_general(lhs, rhs, (((1,), (rhs_dim,)), ((), ())), preferred_element_type=F32)


def loop(count, step):
    if count <= 8:
        for index in range(count):
            step(index)
    else:
        lax.fori_loop(0, count, lambda index, _: (step(index), None)[1], None)


def rotate(x, cosine, sine):
    return x * cosine + pltpu.roll(x, x.shape[-1] // 2, 1) * sine


def kernel(n, heads, chunk, layout_s, layout_v, docs_v, q_hbm, k_ref, v_hbm, g_hbm,
           o_hbm, dq_hbm, dk_out, dv_out,
           q_in, g_in, qe, kall, vall, k_t, v_t, bias_t, cos_ref, sin_ref, probs, o_buf, dq_buf,
           send_buf, recv_buf, own_dv, local_sem, send_sem, recv_sem):
    me = lax.axis_index("context")
    rows, hd = k_ref.shape
    seq = rows * n
    flat = rows * heads
    tokens = chunk // heads
    scale = 1.0 / math.sqrt(hd)

    barrier = pltpu.get_barrier_semaphore()
    for k in range(1, n):
        pl.semaphore_signal(barrier, inc=1, device_id={"context": lax.rem(me + k, n)}, device_id_type=MESH)

    def block(index):
        return pl.ds(pl.multiple_of(index * rows, rows), rows)

    mine = block(me)
    q_copy = pltpu.make_async_copy(q_hbm, q_in, local_sem.at[0])
    g_copy = pltpu.make_async_copy(g_hbm, g_in, local_sem.at[1])
    v_copy = pltpu.make_async_copy(v_hbm, vall.at[mine], local_sem.at[2])
    v_copy.start()
    q_copy.start()
    g_copy.start()

    first = layout_s[me * rows].astype(F32)
    second = layout_s[me * rows + RUN].astype(F32)
    row_at = lax.broadcasted_iota(jnp.int32, (rows, hd), 0)
    token = jnp.where(row_at < RUN, row_at.astype(F32) + first, (row_at - RUN).astype(F32) + second)
    token = token[:, :1]
    docs = jnp.broadcast_to(docs_v[...], (8, seq))
    lane_at = lax.broadcasted_iota(jnp.int32, (8, seq), 1)
    starts = jnp.where(docs != pltpu.roll(docs, 1, 1), lane_at, 0).astype(F32)[:1]
    start = jnp.max(jnp.where(starts <= token, starts, 0.0), axis=1, keepdims=True)
    half = hd // 2
    lane = lax.broadcasted_iota(jnp.int32, (1, hd), 1)
    freq = jnp.exp(-(2.0 * lax.rem(lane, half).astype(F32) / hd) * math.log(THETA))
    angles = (token - start) * freq
    cosine = jnp.cos(angles)
    sine = jnp.where(lane < half, -1.0, 1.0) * jnp.sin(angles)
    cos_ref[...] = cosine
    sin_ref[...] = sine
    kall[mine] = rotate(k_ref[...].astype(F32), cosine, sine).astype(BF16)

    pl.semaphore_wait(barrier, n - 1)

    def transfer(kind, k, source, target):
        return pltpu.make_async_remote_copy(
            src_ref=source, dst_ref=target,
            send_sem=send_sem.at[kind, k], recv_sem=recv_sem.at[kind, k],
            device_id={"context": lax.rem(me + k + 1, n)}, device_id_type=MESH)

    def order(k):
        return (k + 1) % (n - 1) if n <= 8 else k

    def k_send(k):
        return transfer(0, k, kall.at[mine], kall.at[mine])

    def v_send(k):
        return transfer(1, k, vall.at[mine], vall.at[mine])

    def g_send(kind, k):
        return transfer(2 + kind, k, send_buf.at[kind, k], recv_buf.at[kind, k])

    loop(n - 1, lambda k: k_send(k).start())
    v_copy.wait()
    loop(n - 1, lambda k: v_send(k).start())

    keys = layout_v[...].astype(F32)
    bias = jnp.where((keys >= start) & (keys <= token), 0.0, MASKED)
    bias_t[...] = bias.T.astype(BF16)
    q_copy.wait()

    def spread(ref, at):
        part = ref[pl.ds(pl.multiple_of(at * tokens, tokens), tokens), :]
        return jnp.broadcast_to(part[:, None, :], (tokens, heads, hd)).reshape(chunk, hd)

    def span(at):
        return pl.ds(pl.multiple_of(at * chunk, chunk), chunk)

    def make_q(at, _):
        here = span(at)
        qe[here, :hd] = rotate(q_in[here, :].astype(F32), spread(cos_ref, at), spread(sin_ref, at)).astype(BF16)
        row = lax.broadcasted_iota(jnp.int32, (chunk, hd), 0) // heads + at * tokens
        col = lax.broadcasted_iota(jnp.int32, (chunk, hd), 1)
        qe[here, hd:] = (row == col).astype(F32).astype(BF16)

    steps = flat // chunk
    lax.fori_loop(0, steps, make_q, None)
    g_copy.wait()
    loop(n - 1, lambda k: k_send(k).wait_recv())
    k_t[...] = kall[...].astype(F32).T.astype(BF16)

    def make_probs(at, _):
        here = span(at)
        keys_bias = jnp.concatenate([kall[...], bias_t[...]], axis=1)
        scores = dot(keys_bias, qe[here, :], 1)
        largest = jnp.max(scores, axis=0, keepdims=True)
        weights = jnp.exp2((scores - largest) * (scale * math.log2(math.e)))
        total = jnp.sum(weights, axis=0, keepdims=True)
        probs[:, here] = (weights * (1.0 / total)).astype(BF16)

    lax.fori_loop(0, steps, make_probs, None)

    def v_grads(k):
        peer = lax.rem(me + k + 1, n)
        send_buf[0, k] = dot(probs[block(peer), :], g_in[...]).astype(BF16)
        g_send(0, k).start()

    loop(n - 1, v_grads)
    own_dv[...] = dot(probs[mine, :], g_in[...])
    loop(n - 1, lambda k: v_send(k).wait_recv())
    v_t[...] = vall[...].astype(F32).T.astype(BF16)

    def make_ds(at, _):
        here = span(at)
        p_b = probs[:, here]
        o_buf[here, :] = dot(v_t[...], p_b).T.astype(BF16)
        dprobs = dot(vall[...], g_in[here, :], 1)
        p = p_b.astype(F32)
        delta = jnp.sum(p * dprobs, axis=0, keepdims=True)
        probs[:, here] = (p * (dprobs - delta) * scale).astype(BF16)

    lax.fori_loop(0, steps, make_ds, None)
    o_copy = pltpu.make_async_copy(o_buf, o_hbm, local_sem.at[3])
    o_copy.start()

    def k_grads(k):
        peer = lax.rem(me + k + 1, n)
        send_buf[1, k] = dot(probs[block(peer), :], qe[:, :hd]).astype(BF16)
        g_send(1, k).start()

    loop(n - 1, k_grads)
    own_dk = dot(probs[mine, :], qe[:, :hd])

    def make_dq(at, _):
        here = span(at)
        grad = dot(k_t[...], probs[:, here]).T
        dq_buf[here, :] = rotate(grad, spread(cos_ref, at), -spread(sin_ref, at)).astype(BF16)

    lax.fori_loop(0, steps, make_dq, None)
    dq_copy = pltpu.make_async_copy(dq_buf, dq_hbm, local_sem.at[4])
    dq_copy.start()

    def collect(kind, own):
        loop(n - 1, lambda k: g_send(kind, k).wait_recv())
        return own + jnp.sum(recv_buf[kind].astype(F32), axis=0)

    dv_out[...] = collect(0, own_dv[...])
    dk_out[...] = rotate(collect(1, own_dk), cos_ref[...], -sin_ref[...])

    def finish(k):
        k_send(k).wait_send()
        v_send(k).wait_send()
        g_send(0, k).wait_send()
        g_send(1, k).wait_send()

    loop(n - 1, finish)
    o_copy.wait()
    dq_copy.wait()


def body(n, queries, key_heads, value_heads, out_grad, layout, documents):
    rows, heads, hd = queries.shape
    seq = layout.shape[0]
    flat = rows * heads
    chunk = 256 if seq <= 1024 else 128
    any_spec = pl.BlockSpec(memory_space=pl.ANY)
    vmem_spec = pl.BlockSpec(memory_space=pltpu.VMEM)
    out, dq, dk, dv = pl.pallas_call(
        functools.partial(kernel, n, heads, chunk),
        out_shape=(
            jax.ShapeDtypeStruct((flat, hd), BF16),
            jax.ShapeDtypeStruct((flat, hd), BF16),
            jax.ShapeDtypeStruct((rows, hd), F32),
            jax.ShapeDtypeStruct((rows, hd), F32),
        ),
        in_specs=[pl.BlockSpec(memory_space=pltpu.SMEM), vmem_spec, vmem_spec,
                  any_spec, vmem_spec, any_spec, any_spec],
        out_specs=(any_spec, any_spec, vmem_spec, vmem_spec),
        scratch_shapes=[
            pltpu.VMEM((flat, hd), BF16),
            pltpu.VMEM((flat, hd), BF16),
            pltpu.VMEM((flat, 2 * hd), BF16),
            pltpu.VMEM((seq, hd), BF16),
            pltpu.VMEM((seq, hd), BF16),
            pltpu.VMEM((hd, seq), BF16),
            pltpu.VMEM((hd, seq), BF16),
            pltpu.VMEM((seq, rows), BF16),
            pltpu.VMEM((rows, hd), F32),
            pltpu.VMEM((rows, hd), F32),
            pltpu.VMEM((seq, flat), BF16),
            pltpu.VMEM((flat, hd), BF16),
            pltpu.VMEM((flat, hd), BF16),
            pltpu.VMEM((2, n - 1, rows, hd), BF16),
            pltpu.VMEM((2, n - 1, rows, hd), BF16),
            pltpu.VMEM((rows, hd), F32),
            pltpu.SemaphoreType.DMA((5,)),
            pltpu.SemaphoreType.DMA((4, n - 1)),
            pltpu.SemaphoreType.DMA((4, n - 1)),
        ],
        compiler_params=pltpu.CompilerParams(
            collective_id=0, has_side_effects=True, vmem_limit_bytes=52 * 1024 * 1024),
    )(
        layout, layout.reshape(1, seq), documents.reshape(1, seq),
        queries.reshape(flat, hd), key_heads.reshape(rows, hd), value_heads.reshape(rows, hd),
        out_grad.reshape(flat, hd),
    )
    return (out.reshape(rows, heads, hd), dq.reshape(rows, heads, hd), dk, dv)


def solution(mesh):
    return jax.shard_map(
        functools.partial(body, mesh.shape["context"]),
        mesh=mesh,
        in_specs=(
            P(("dp", "context"), "tensor", None),
            P(("dp", "context"), "tensor", None),
            P(("dp", "context"), "tensor", None),
            P(("dp", "context"), "tensor", None),
            P("dp"),
            P("dp"),
        ),
        out_specs=(
            P(("dp", "context"), "tensor", None),
            P(("dp", "context"), "tensor", None),
            P(("dp", "context"), "tensor"),
            P(("dp", "context"), "tensor"),
        ),
        check_vma=False,
    )
```

```python
import functools
import math

import jax
import jax.numpy as jnp
from jax import lax
from jax.experimental import pallas as pl
from jax.experimental.pallas import tpu as pltpu
from jax.sharding import PartitionSpec as P

THETA = 8000000.0
RUN = 64
MASKED = -1e30
MESH = pl.DeviceIdType.MESH
F32 = jnp.float32
BF16 = jnp.bfloat16


def dot(lhs, rhs, rhs_dim=0):
    return lax.dot_general(lhs, rhs, (((1,), (rhs_dim,)), ((), ())), preferred_element_type=F32)


def loop(count, step):
    if count <= 8:
        for index in range(count):
            step(index)
    else:
        lax.fori_loop(0, count, lambda index, _: (step(index), None)[1], None)


def span(at, size):
    start = at * size
    return pl.ds(start if isinstance(at, int) else pl.multiple_of(start, size), size)


def rotate(x, cosine, sine):
    return x * cosine + pltpu.roll(x, x.shape[-1] // 2, 1) * sine


def spread(ref, at, chunk, heads):
    part = ref[span(at, chunk // heads), :]
    return jnp.broadcast_to(part[:, None, :], (chunk // heads, heads, part.shape[-1])).reshape(chunk, -1)


def main_kernel(n, heads, chunk, layout_h, layout_row_h, docs_h, q_h, k_h, v_h, g_h,
                o_ref, probs, k_t, cos_ref, sin_ref, dk_ref, dv_ref,
                layout_s, layout_v, docs_v, k_in, q_in, g_in, qe, kall, vall, v_t, p_t, bias_t,
                send_buf, recv_buf, own_dv, local_sem, send_sem, recv_sem):
    me = lax.axis_index("context")
    rows, hd = k_in.shape
    seq = rows * n
    flat = rows * heads
    tokens = chunk // heads
    steps = flat // chunk
    scale = 1.0 / math.sqrt(hd)

    barrier = pltpu.get_barrier_semaphore()
    for k in range(1, n):
        pl.semaphore_signal(barrier, inc=1, device_id={"context": lax.rem(me + k, n)}, device_id_type=MESH)

    mine = span(me, rows)
    layout_copy = pltpu.make_async_copy(layout_h, layout_s, local_sem.at[0])
    docs_copy = pltpu.make_async_copy(docs_h, docs_v, local_sem.at[1])
    k_copy = pltpu.make_async_copy(k_h, k_in, local_sem.at[2])
    row_copy = pltpu.make_async_copy(layout_row_h, layout_v, local_sem.at[3])
    v_copy = pltpu.make_async_copy(v_h, vall.at[mine], local_sem.at[4])
    q_copy = pltpu.make_async_copy(q_h, q_in, local_sem.at[5])
    g_copy = pltpu.make_async_copy(g_h, g_in, local_sem.at[6])
    for copy in (layout_copy, docs_copy, k_copy, v_copy, row_copy, q_copy, g_copy):
        copy.start()

    half = hd // 2
    lane = lax.broadcasted_iota(jnp.int32, (1, hd), 1)
    freq = jnp.exp(-(2.0 * lax.rem(lane, half).astype(F32) / hd) * math.log(THETA))
    row_at = lax.broadcasted_iota(jnp.int32, (rows, hd), 0)
    layout_copy.wait()
    first = layout_s[me * rows].astype(F32)
    second = layout_s[me * rows + RUN].astype(F32)
    token = jnp.where(row_at < RUN, row_at.astype(F32) + first, (row_at - RUN).astype(F32) + second)
    token = token[:, :1]
    docs_copy.wait()
    docs = jnp.broadcast_to(docs_v[...], (8, seq))
    lane_at = lax.broadcasted_iota(jnp.int32, (8, seq), 1)
    starts = jnp.where(docs != pltpu.roll(docs, 1, 1), lane_at, 0).astype(F32)[:1]
    start = jnp.max(jnp.where(starts <= token, starts, 0.0), axis=1, keepdims=True)
    angles = (token - start) * freq
    cosine = jnp.cos(angles)
    sine = jnp.where(lane < half, -1.0, 1.0) * jnp.sin(angles)
    cos_ref[...] = cosine
    sin_ref[...] = sine
    k_copy.wait()
    kall[mine] = rotate(k_in[...].astype(F32), cosine, sine).astype(BF16)
    v_copy.wait()

    pl.semaphore_wait(barrier, n - 1)

    def transfer(kind, k, source, target):
        return pltpu.make_async_remote_copy(
            src_ref=source, dst_ref=target,
            send_sem=send_sem.at[kind, k], recv_sem=recv_sem.at[kind, k],
            device_id={"context": lax.rem(me + k + 1, n)}, device_id_type=MESH)

    def k_send(k):
        return transfer(0, k, kall.at[mine], kall.at[mine])

    def v_send(k):
        return transfer(1, k, vall.at[mine], vall.at[mine])

    def g_send(kind, k):
        return transfer(2 + kind, k, send_buf.at[kind, k], recv_buf.at[kind, k])

    loop(n - 1, lambda k: k_send(k).start())
    loop(n - 1, lambda k: v_send(k).start())

    row_copy.wait()
    keys = layout_v[...].astype(F32)
    bias_t[...] = jnp.where((keys >= start) & (keys <= token), 0.0, MASKED).T.astype(BF16)
    q_copy.wait()

    def make_q(at):
        here = span(at, chunk)
        cosines, sines = spread(cos_ref, at, chunk, heads), spread(sin_ref, at, chunk, heads)
        qe[here, :hd] = rotate(q_in[here, :].astype(F32), cosines, sines).astype(BF16)
        row = lax.broadcasted_iota(jnp.int32, (chunk, hd), 0) // heads + at * tokens
        col = lax.broadcasted_iota(jnp.int32, (chunk, hd), 1)
        qe[here, hd:] = (row == col).astype(F32).astype(BF16)

    loop(steps, make_q)
    g_copy.wait()
    loop(n - 1, lambda k: k_send(k).wait_recv())
    k_t[...] = kall[...].astype(F32).T.astype(BF16)

    def make_probs(at):
        here = span(at, chunk)
        scores = dot(jnp.concatenate([kall[...], bias_t[...]], axis=1), qe[here, :], 1)
        largest = jnp.max(scores, axis=0, keepdims=True)
        weights = jnp.exp2((scores - largest) * (scale * math.log2(math.e)))
        total = jnp.sum(weights, axis=0, keepdims=True)
        p_t[:, here] = (weights * (1.0 / total)).astype(BF16)

    loop(steps, make_probs)

    def v_grads(k):
        send_buf[0, k] = dot(p_t[span(lax.rem(me + k + 1, n), rows), :], g_in[...]).astype(BF16)
        g_send(0, k).start()

    loop(n - 1, v_grads)
    own_dv[...] = dot(p_t[mine, :], g_in[...])
    loop(n - 1, lambda k: v_send(k).wait_recv())

    def make_ds(at):
        here = span(at, chunk)
        dprobs = dot(vall[...], g_in[here, :], 1)
        p = p_t[:, here].astype(F32)
        delta = jnp.sum(p * dprobs, axis=0, keepdims=True)
        probs[:, here] = (p * (dprobs - delta) * scale).astype(BF16)

    loop(steps, make_ds)

    def k_grads(k):
        send_buf[1, k] = dot(probs[span(lax.rem(me + k + 1, n), rows), :], qe[:, :hd]).astype(BF16)
        g_send(1, k).start()

    loop(n - 1, k_grads)
    own_dk = dot(probs[mine, :], qe[:, :hd])
    v_t[...] = vall[...].astype(F32).T.astype(BF16)

    def make_o(at):
        here = span(at, chunk)
        o_ref[here, :] = dot(v_t[...], p_t[:, here]).T.astype(BF16)

    loop(steps, make_o)

    def collect(kind, own):
        loop(n - 1, lambda k: g_send(kind, k).wait_recv())
        return own + jnp.sum(recv_buf[kind].astype(F32), axis=0)

    dv_ref[...] = collect(0, own_dv[...])
    dk_ref[...] = rotate(collect(1, own_dk), cos_ref[...], -sin_ref[...])

    def finish(k):
        k_send(k).wait_send()
        v_send(k).wait_send()
        g_send(0, k).wait_send()
        g_send(1, k).wait_send()

    loop(n - 1, finish)


def last_kernel(heads, chunk, parts, o_ref, probs, k_t, cos_ref, sin_ref, dk_ref, dv_ref,
                o_h, dq_h, dk_h, dv_h, dq_buf, sem):
    flat = dq_buf.shape[0]
    copies = [pltpu.make_async_copy(src, dst, sem.at[at])
              for at, (src, dst) in enumerate(((o_ref, o_h), (dk_ref, dk_h), (dv_ref, dv_h)))]
    for copy in copies:
        copy.start()

    def make_dq(at):
        here = span(at, chunk)
        grad = dot(k_t[...], probs[:, here]).T
        cosines, sines = spread(cos_ref, at, chunk, heads), spread(sin_ref, at, chunk, heads)
        dq_buf[here, :] = rotate(grad, cosines, -sines).astype(BF16)

    steps = flat // chunk // parts
    for part in range(parts):
        loop(steps, lambda at, part=part: make_dq(at + part * steps))
        where = span(part, flat // parts)
        copy = pltpu.make_async_copy(dq_buf.at[where], dq_h.at[where], sem.at[3 + part])
        copy.start()
        copies.append(copy)
    for copy in copies:
        copy.wait()


def body(n, queries, key_heads, value_heads, out_grad, layout, documents):
    rows, heads, hd = queries.shape
    seq = layout.shape[0]
    flat = rows * heads
    small = seq <= 1024
    chunk = 256 if small else 128
    parts = 4
    hbm = pl.BlockSpec(memory_space=pltpu.HBM)
    vmem = pl.BlockSpec(memory_space=pltpu.VMEM)
    carried = pl.pallas_call(
        functools.partial(main_kernel, n, heads, chunk),
        out_shape=(
            jax.ShapeDtypeStruct((flat, hd), BF16),
            jax.ShapeDtypeStruct((seq, flat), BF16),
            jax.ShapeDtypeStruct((hd, seq), BF16),
            jax.ShapeDtypeStruct((rows, hd), F32),
            jax.ShapeDtypeStruct((rows, hd), F32),
            jax.ShapeDtypeStruct((rows, hd), F32),
            jax.ShapeDtypeStruct((rows, hd), F32),
        ),
        in_specs=[hbm] * 7,
        out_specs=(vmem,) * 7,
        scratch_shapes=[
            pltpu.SMEM((seq,), jnp.int32),
            pltpu.VMEM((1, seq), jnp.int32),
            pltpu.VMEM((1, seq), jnp.int32),
            pltpu.VMEM((rows, hd), BF16),
            pltpu.VMEM((flat, hd), BF16),
            pltpu.VMEM((flat, hd), BF16),
            pltpu.VMEM((flat, 2 * hd), BF16),
            pltpu.VMEM((seq, hd), BF16),
            pltpu.VMEM((seq, hd), BF16),
            pltpu.VMEM((hd, seq), BF16),
            pltpu.VMEM((seq, flat), BF16),
            pltpu.VMEM((seq, rows), BF16),
            pltpu.VMEM((2, n - 1, rows, hd), BF16),
            pltpu.VMEM((2, n - 1, rows, hd), BF16),
            pltpu.VMEM((rows, hd), F32),
            pltpu.SemaphoreType.DMA((7,)),
            pltpu.SemaphoreType.DMA((4, n - 1)),
            pltpu.SemaphoreType.DMA((4, n - 1)),
        ],
        compiler_params=pltpu.CompilerParams(
            collective_id=0, has_side_effects=True, vmem_limit_bytes=(32 if small else 50) * 1024 * 1024),
    )(*[pltpu.with_memory_space_constraint(operand, pltpu.HBM) for operand in (
        layout, layout.reshape(1, seq), documents.reshape(1, seq),
        queries.reshape(flat, hd), key_heads.reshape(rows, hd), value_heads.reshape(rows, hd),
        out_grad.reshape(flat, hd),
    )])
    out, dq, dk, dv = pl.pallas_call(
        functools.partial(last_kernel, heads, chunk, parts),
        out_shape=(
            jax.ShapeDtypeStruct((flat, hd), BF16),
            jax.ShapeDtypeStruct((flat, hd), BF16),
            jax.ShapeDtypeStruct((rows, hd), F32),
            jax.ShapeDtypeStruct((rows, hd), F32),
        ),
        in_specs=[vmem] * 7,
        out_specs=(hbm,) * 4,
        scratch_shapes=[pltpu.VMEM((flat, hd), BF16), pltpu.SemaphoreType.DMA((3 + parts,))],
        compiler_params=pltpu.CompilerParams(vmem_limit_bytes=(16 if small else 40) * 1024 * 1024),
    )(*carried)
    return (out.reshape(rows, heads, hd), dq.reshape(rows, heads, hd), dk, dv)


def solution(mesh):
    return jax.shard_map(
        functools.partial(body, mesh.shape["context"]),
        mesh=mesh,
        in_specs=(
            P(("dp", "context"), "tensor", None),
            P(("dp", "context"), "tensor", None),
            P(("dp", "context"), "tensor", None),
            P(("dp", "context"), "tensor", None),
            P("dp"),
            P("dp"),
        ),
        out_specs=(
            P(("dp", "context"), "tensor", None),
            P(("dp", "context"), "tensor", None),
            P(("dp", "context"), "tensor"),
            P(("dp", "context"), "tensor"),
        ),
        check_vma=False,
    )
```

```python
import functools
import math

import jax
import jax.numpy as jnp
from jax import lax
from jax.experimental import pallas as pl
from jax.experimental.pallas import tpu as pltpu
from jax.sharding import PartitionSpec as P

THETA = 8000000.0
RUN = 64
MASKED = -1e30
MESH = pl.DeviceIdType.MESH
F32 = jnp.float32
BF16 = jnp.bfloat16


def dot(lhs, rhs, rhs_dim=0):
    return lax.dot_general(lhs, rhs, (((1,), (rhs_dim,)), ((), ())), preferred_element_type=F32)


def loop(count, step):
    if count <= 8:
        for index in range(count):
            step(index)
    else:
        lax.fori_loop(0, count, lambda index, _: (step(index), None)[1], None)


def span(at, size):
    start = at * size
    return pl.ds(start if isinstance(at, int) else pl.multiple_of(start, size), size)


def rotate(x, cosine, sine):
    return x * cosine + pltpu.roll(x, x.shape[-1] // 2, 1) * sine


def spread(ref, at, chunk, heads):
    part = ref[span(at, chunk // heads), :]
    return jnp.broadcast_to(part[:, None, :], (chunk // heads, heads, part.shape[-1])).reshape(chunk, -1)


def main_kernel(n, heads, chunk, layout_h, layout_row_h, docs_h, q_h, k_h, v_h, g_h,
                o_ref, dq_ref, dk_ref, dv_ref,
                probs, k_t, cos_ref, sin_ref, w_near, stats, layout_s, layout_v, docs_v, k_in, q_in, g_in, qe, kall, vall, v_t, p_t, bias_t,
                send_buf, recv_buf, own_dv, local_sem, send_sem, recv_sem):
    me = lax.axis_index("context")
    rows, hd = k_in.shape
    seq = rows * n
    flat = rows * heads
    tokens = chunk // heads
    steps = flat // chunk
    scale = 1.0 / math.sqrt(hd)

    factor = scale * math.log2(math.e)

    def peer(k):
        pair = lax.rem(me // 2 + (k + 1) // 2, n // 2)
        return pair * 2 + lax.rem(me + k + 1, 2)

    barrier = pltpu.get_barrier_semaphore()
    for k in range(n - 1):
        pl.semaphore_signal(barrier, inc=1, device_id={"context": peer(k)}, device_id_type=MESH)

    mine = span(me, rows)
    layout_copy = pltpu.make_async_copy(layout_h, layout_s, local_sem.at[0])
    docs_copy = pltpu.make_async_copy(docs_h, docs_v, local_sem.at[1])
    k_copy = pltpu.make_async_copy(k_h, k_in, local_sem.at[2])
    row_copy = pltpu.make_async_copy(layout_row_h, layout_v, local_sem.at[3])
    v_copy = pltpu.make_async_copy(v_h, vall.at[mine], local_sem.at[4])
    q_copy = pltpu.make_async_copy(q_h, q_in, local_sem.at[5])
    g_copy = pltpu.make_async_copy(g_h, g_in, local_sem.at[6])
    for copy in (layout_copy, docs_copy, k_copy, v_copy, row_copy, q_copy, g_copy):
        copy.start()

    half = hd // 2
    lane = lax.broadcasted_iota(jnp.int32, (1, hd), 1)
    freq = jnp.exp(-(2.0 * lax.rem(lane, half).astype(F32) / hd) * math.log(THETA))
    row_at = lax.broadcasted_iota(jnp.int32, (rows, hd), 0)
    layout_copy.wait()
    first = layout_s[me * rows].astype(F32)
    second = layout_s[me * rows + RUN].astype(F32)
    token = jnp.where(row_at < RUN, row_at.astype(F32) + first, (row_at - RUN).astype(F32) + second)
    token = token[:, :1]
    docs_copy.wait()
    docs = jnp.broadcast_to(docs_v[...], (8, seq))
    lane_at = lax.broadcasted_iota(jnp.int32, (8, seq), 1)
    starts = jnp.where(docs != pltpu.roll(docs, 1, 1), lane_at, 0).astype(F32)[:1]
    start = jnp.max(jnp.where(starts <= token, starts, 0.0), axis=1, keepdims=True)
    angles = (token - start) * freq
    cosine = jnp.cos(angles)
    sine = jnp.where(lane < half, -1.0, 1.0) * jnp.sin(angles)
    cos_ref[...] = cosine
    sin_ref[...] = sine
    k_copy.wait()
    kall[mine] = rotate(k_in[...].astype(F32), cosine, sine).astype(BF16)
    v_copy.wait()

    pl.semaphore_wait(barrier, n - 1)

    def transfer(kind, k, source, target):
        return pltpu.make_async_remote_copy(
            src_ref=source, dst_ref=target,
            send_sem=send_sem.at[kind, k], recv_sem=recv_sem.at[kind, k],
            device_id={"context": peer(k)}, device_id_type=MESH)

    def k_send(k):
        return transfer(0, k, kall.at[mine], kall.at[mine])

    def v_send(k):
        return transfer(1, k, vall.at[mine], vall.at[mine])

    def g_send(kind, k):
        return transfer(2 + kind, k, send_buf.at[kind, k], recv_buf.at[kind, k])

    loop(n - 1, lambda k: k_send(n - 2 - k).start())

    row_copy.wait()
    keys = layout_v[...].astype(F32)
    bias_t[...] = jnp.where((keys >= start) & (keys <= token), 0.0, MASKED).T.astype(BF16)
    q_copy.wait()

    def make_q(at):
        here = span(at, chunk)
        cosines, sines = spread(cos_ref, at, chunk, heads), spread(sin_ref, at, chunk, heads)
        qe[here, :hd] = rotate(q_in[here, :].astype(F32), cosines, sines).astype(BF16)
        row = lax.broadcasted_iota(jnp.int32, (chunk, hd), 0) // heads + at * tokens
        col = lax.broadcasted_iota(jnp.int32, (chunk, hd), 1)
        qe[here, hd:] = (row == col).astype(F32).astype(BF16)

    loop(steps, make_q)

    def make_probs(at):
        here = span(at, chunk)
        scores = dot(jnp.concatenate([kall[...], bias_t[...]], axis=1), qe[here, :], 1)
        largest = jnp.max(scores, axis=0, keepdims=True)
        weights = jnp.exp2((scores - largest) * factor)
        total = jnp.sum(weights, axis=0, keepdims=True)
        p_t[:, here] = (weights * (1.0 / total)).astype(BF16)

    near = span(me // 2, 2 * rows)
    far = span(1 - me // 2, 2 * rows)

    def make_near(at):
        here = span(at, chunk)
        scores = dot(jnp.concatenate([kall[near, :], bias_t[near, :]], axis=1), qe[here, :], 1)
        largest = jnp.max(scores, axis=0, keepdims=True)
        weights = jnp.exp2((scores - largest) * factor)
        w_near[:, here] = weights
        stats[0:1, here] = largest
        stats[1:2, here] = jnp.sum(weights, axis=0, keepdims=True)

    def make_far(at):
        here = span(at, chunk)
        scores = dot(jnp.concatenate([kall[far, :], bias_t[far, :]], axis=1), qe[here, :], 1)
        near_largest = stats[0:1, here]
        largest = jnp.maximum(near_largest, jnp.max(scores, axis=0, keepdims=True))
        weights = jnp.exp2((scores - largest) * factor)
        shrink = jnp.exp2((near_largest - largest) * factor)
        inverse = 1.0 / (stats[1:2, here] * shrink + jnp.sum(weights, axis=0, keepdims=True))
        p_t[far, here] = (weights * inverse).astype(BF16)
        p_t[near, here] = (w_near[:, here] * (shrink * inverse)).astype(BF16)

    if n == 4:
        k_send(0).wait_recv()
        loop(steps, make_near)
        k_send(1).wait_recv()
        k_send(2).wait_recv()
        loop(n - 1, lambda k: v_send(n - 2 - k).start())
        loop(steps, make_far)
    else:
        loop(n - 1, lambda k: k_send(k).wait_recv())
        loop(n - 1, lambda k: v_send(k).start())
        loop(steps, make_probs)
    g_copy.wait()

    def v_grads(k):
        send_buf[0, k] = dot(p_t[span(peer(k), rows), :], g_in[...]).astype(BF16)
        g_send(0, k).start()

    loop(n - 1, lambda k: v_grads(n - 2 - k))
    loop(n - 1, lambda k: v_send(k).wait_recv())

    def make_ds(at):
        here = span(at, chunk)
        dprobs = dot(vall[...], g_in[here, :], 1)
        p = p_t[:, here].astype(F32)
        delta = jnp.sum(p * dprobs, axis=0, keepdims=True)
        probs[:, here] = (p * (dprobs - delta)).astype(BF16)

    loop(steps, make_ds)

    def k_grads(k):
        send_buf[1, k] = (dot(probs[span(peer(k), rows), :], qe[:, :hd]) * scale).astype(BF16)
        g_send(1, k).start()

    loop(n - 1, lambda k: k_grads(n - 2 - k))
    own_dk = dot(probs[mine, :], qe[:, :hd]) * scale
    own_dv[...] = dot(p_t[mine, :], g_in[...])
    k_t[...] = kall[...].astype(F32).T.astype(BF16)
    v_t[...] = vall[...].astype(F32).T.astype(BF16)

    def make_o(at):
        here = span(at, chunk)
        o_ref[here, :] = dot(v_t[...], p_t[:, here]).T.astype(BF16)

    def make_dq(at):
        here = span(at, chunk)
        grad = dot(k_t[...], probs[:, here]).T * scale
        cosines, sines = spread(cos_ref, at, chunk, heads), spread(sin_ref, at, chunk, heads)
        dq_ref[here, :] = rotate(grad, cosines, -sines).astype(BF16)

    loop(steps, make_o)
    loop(steps, make_dq)

    def collect(kind, own):
        loop(n - 1, lambda k: g_send(kind, k).wait_recv())
        return own + jnp.sum(recv_buf[kind].astype(F32), axis=0)

    dv_ref[...] = collect(0, own_dv[...])
    dk_ref[...] = rotate(collect(1, own_dk), cos_ref[...], -sin_ref[...])

    def finish(k):
        k_send(k).wait_send()
        v_send(k).wait_send()
        g_send(0, k).wait_send()
        g_send(1, k).wait_send()

    loop(n - 1, finish)


def last_kernel(*refs):
    count = len(refs) // 2
    sem = refs[-1]
    copies = [pltpu.make_async_copy(refs[at], refs[count + at], sem.at[at]) for at in range(count)]
    for copy in copies:
        copy.start()
    for copy in copies:
        copy.wait()


def body(n, queries, key_heads, value_heads, out_grad, layout, documents):
    rows, heads, hd = queries.shape
    seq = layout.shape[0]
    flat = rows * heads
    small = seq <= 1024
    chunk = 256 if small else 128
    hbm = pl.BlockSpec(memory_space=pltpu.HBM)
    vmem = pl.BlockSpec(memory_space=pltpu.VMEM)
    shapes = (
        jax.ShapeDtypeStruct((flat, hd), BF16),
        jax.ShapeDtypeStruct((flat, hd), BF16),
        jax.ShapeDtypeStruct((rows, hd), F32),
        jax.ShapeDtypeStruct((rows, hd), F32),
    )
    carried = pl.pallas_call(
        functools.partial(main_kernel, n, heads, chunk),
        out_shape=shapes,
        in_specs=[hbm] * 7,
        out_specs=(vmem,) * 4,
        scratch_shapes=[
            pltpu.VMEM((seq, flat), BF16),
            pltpu.VMEM((hd, seq), BF16),
            pltpu.VMEM((rows, hd), F32),
            pltpu.VMEM((rows, hd), F32),
            pltpu.VMEM((2 * rows if n == 4 else 8, flat), F32),
            pltpu.VMEM((8, flat), F32),
            pltpu.SMEM((seq,), jnp.int32),
            pltpu.VMEM((1, seq), jnp.int32),
            pltpu.VMEM((1, seq), jnp.int32),
            pltpu.VMEM((rows, hd), BF16),
            pltpu.VMEM((flat, hd), BF16),
            pltpu.VMEM((flat, hd), BF16),
            pltpu.VMEM((flat, 2 * hd), BF16),
            pltpu.VMEM((seq, hd), BF16),
            pltpu.VMEM((seq, hd), BF16),
            pltpu.VMEM((hd, seq), BF16),
            pltpu.VMEM((seq, flat), BF16),
            pltpu.VMEM((seq, rows), BF16),
            pltpu.VMEM((2, n - 1, rows, hd), BF16),
            pltpu.VMEM((2, n - 1, rows, hd), BF16),
            pltpu.VMEM((rows, hd), F32),
            pltpu.SemaphoreType.DMA((7,)),
            pltpu.SemaphoreType.DMA((4, n - 1)),
            pltpu.SemaphoreType.DMA((4, n - 1)),
        ],
        compiler_params=pltpu.CompilerParams(
            collective_id=0, has_side_effects=True, vmem_limit_bytes=(40 if small else 58) * 1024 * 1024),
    )(*[pltpu.with_memory_space_constraint(operand, pltpu.HBM) for operand in (
        layout, layout.reshape(1, seq), documents.reshape(1, seq),
        queries.reshape(flat, hd), key_heads.reshape(rows, hd), value_heads.reshape(rows, hd),
        out_grad.reshape(flat, hd),
    )])
    out, dq, dk, dv = pl.pallas_call(
        last_kernel,
        out_shape=shapes,
        in_specs=[vmem] * 4,
        out_specs=(hbm,) * 4,
        scratch_shapes=[pltpu.SemaphoreType.DMA((4,))],
        compiler_params=pltpu.CompilerParams(vmem_limit_bytes=8 * 1024 * 1024),
    )(*carried)
    return (out.reshape(rows, heads, hd), dq.reshape(rows, heads, hd), dk, dv)


def solution(mesh):
    return jax.shard_map(
        functools.partial(body, mesh.shape["context"]),
        mesh=mesh,
        in_specs=(
            P(("dp", "context"), "tensor", None),
            P(("dp", "context"), "tensor", None),
            P(("dp", "context"), "tensor", None),
            P(("dp", "context"), "tensor", None),
            P("dp"),
            P("dp"),
        ),
        out_specs=(
            P(("dp", "context"), "tensor", None),
            P(("dp", "context"), "tensor", None),
            P(("dp", "context"), "tensor"),
            P(("dp", "context"), "tensor"),
        ),
        check_vma=False,
    )
```

```python
import functools
import math

import jax
import jax.numpy as jnp
from jax import lax
from jax.experimental import pallas as pl
from jax.experimental.pallas import tpu as pltpu
from jax.sharding import PartitionSpec as P

THETA = 8000000.0
RUN = 64
MASKED = -1e30
MESH = pl.DeviceIdType.MESH
F32 = jnp.float32
BF16 = jnp.bfloat16


def dot(lhs, rhs, rhs_dim=0):
    return lax.dot_general(lhs, rhs, (((1,), (rhs_dim,)), ((), ())), preferred_element_type=F32)


def loop(count, step):
    if count <= 8:
        for index in range(count):
            step(index)
    else:
        lax.fori_loop(0, count, lambda index, _: (step(index), None)[1], None)


def span(at, size):
    start = at * size
    return pl.ds(start if isinstance(at, int) else pl.multiple_of(start, size), size)


def rotate(x, cosine, sine):
    return x * cosine + pltpu.roll(x, x.shape[-1] // 2, 1) * sine


def spread(ref, at, chunk, heads):
    part = ref[span(at, chunk // heads), :]
    return jnp.broadcast_to(part[:, None, :], (chunk // heads, heads, part.shape[-1])).reshape(chunk, -1)


def main_kernel(n, heads, chunk, layout_h, layout_row_h, docs_h, q_h, k_h, v_h, g_h,
                o_ref, dq_ref, dk_ref, dv_ref,
                probs, k_t, cos_ref, sin_ref, w_near, stats, layout_s, layout_v, docs_v, k_in, q_in, g_in, qe, kall, vall, v_t, p_t, bias_t,
                send_buf, recv_buf, own_dv, local_sem, send_sem, recv_sem):
    me = lax.axis_index("context")
    rows, hd = k_in.shape
    seq = rows * n
    flat = rows * heads
    tokens = chunk // heads
    steps = flat // chunk
    scale = 1.0 / math.sqrt(hd)

    factor = scale * math.log2(math.e)

    def peer(k):
        pair = lax.rem(me // 2 + (k + 1) // 2, n // 2)
        return pair * 2 + lax.rem(me + k + 1, 2)

    barrier = pltpu.get_barrier_semaphore()
    for k in range(n - 1):
        pl.semaphore_signal(barrier, inc=1, device_id={"context": peer(k)}, device_id_type=MESH)

    mine = span(me, rows)
    layout_copy = pltpu.make_async_copy(layout_h, layout_s, local_sem.at[0])
    docs_copy = pltpu.make_async_copy(docs_h, docs_v, local_sem.at[1])
    k_copy = pltpu.make_async_copy(k_h, k_in, local_sem.at[2])
    row_copy = pltpu.make_async_copy(layout_row_h, layout_v, local_sem.at[3])
    v_copy = pltpu.make_async_copy(v_h, vall.at[mine], local_sem.at[4])
    q_copy = pltpu.make_async_copy(q_h, q_in, local_sem.at[5])
    g_copy = pltpu.make_async_copy(g_h, g_in, local_sem.at[6])
    for copy in (layout_copy, docs_copy, k_copy, v_copy, row_copy, q_copy, g_copy):
        copy.start()

    half = hd // 2
    lane = lax.broadcasted_iota(jnp.int32, (1, hd), 1)
    freq = jnp.exp(-(2.0 * lax.rem(lane, half).astype(F32) / hd) * math.log(THETA))
    row_at = lax.broadcasted_iota(jnp.int32, (rows, hd), 0)
    layout_copy.wait()
    first = layout_s[me * rows].astype(F32)
    second = layout_s[me * rows + RUN].astype(F32)
    token = jnp.where(row_at < RUN, row_at.astype(F32) + first, (row_at - RUN).astype(F32) + second)
    token = token[:, :1]
    docs_copy.wait()
    docs = jnp.broadcast_to(docs_v[...], (8, seq))
    lane_at = lax.broadcasted_iota(jnp.int32, (8, seq), 1)
    starts = jnp.where(docs != pltpu.roll(docs, 1, 1), lane_at, 0).astype(F32)[:1]
    start = jnp.max(jnp.where(starts <= token, starts, 0.0), axis=1, keepdims=True)
    angles = (token - start) * freq
    cosine = jnp.cos(angles)
    sine = jnp.where(lane < half, -1.0, 1.0) * jnp.sin(angles)
    cos_ref[...] = cosine
    sin_ref[...] = sine
    k_copy.wait()
    kall[mine] = rotate(k_in[...].astype(F32), cosine, sine).astype(BF16)
    v_copy.wait()

    pl.semaphore_wait(barrier, n - 1)

    def transfer(kind, k, source, target):
        return pltpu.make_async_remote_copy(
            src_ref=source, dst_ref=target,
            send_sem=send_sem.at[kind, k], recv_sem=recv_sem.at[kind, k],
            device_id={"context": peer(k)}, device_id_type=MESH)

    def k_send(k):
        return transfer(0, k, kall.at[mine], kall.at[mine])

    def v_send(k):
        return transfer(1, k, vall.at[mine], vall.at[mine])

    def g_send(kind, k):
        return transfer(2 + kind, k, send_buf.at[kind, k], recv_buf.at[kind, k])

    loop(n - 1, lambda k: k_send(n - 2 - k).start())
    if n == 4:
        loop(n - 1, lambda k: v_send(n - 2 - k).start())

    row_copy.wait()
    keys = layout_v[...].astype(F32)
    bias_t[...] = jnp.where((keys >= start) & (keys <= token), 0.0, MASKED).T.astype(BF16)
    q_copy.wait()

    def make_q(at):
        here = span(at, chunk)
        cosines, sines = spread(cos_ref, at, chunk, heads), spread(sin_ref, at, chunk, heads)
        qe[here, :hd] = rotate(q_in[here, :].astype(F32), cosines, sines).astype(BF16)
        row = lax.broadcasted_iota(jnp.int32, (chunk, hd), 0) // heads + at * tokens
        col = lax.broadcasted_iota(jnp.int32, (chunk, hd), 1)
        qe[here, hd:] = (row == col).astype(F32).astype(BF16)

    loop(steps, make_q)

    def make_probs(at):
        here = span(at, chunk)
        scores = dot(jnp.concatenate([kall[...], bias_t[...]], axis=1), qe[here, :], 1)
        largest = jnp.max(scores, axis=0, keepdims=True)
        weights = jnp.exp2((scores - largest) * factor)
        total = jnp.sum(weights, axis=0, keepdims=True)
        p_t[:, here] = (weights * (1.0 / total)).astype(BF16)

    near = span(me // 2, 2 * rows)
    far = span(1 - me // 2, 2 * rows)

    def make_near(at):
        here = span(at, chunk)
        scores = dot(jnp.concatenate([kall[near, :], bias_t[near, :]], axis=1), qe[here, :], 1)
        largest = jnp.max(scores, axis=0, keepdims=True)
        weights = jnp.exp2((scores - largest) * factor)
        w_near[:, here] = weights
        stats[0:1, here] = largest
        stats[1:2, here] = jnp.sum(weights, axis=0, keepdims=True)

    def make_far(at):
        here = span(at, chunk)
        scores = dot(jnp.concatenate([kall[far, :], bias_t[far, :]], axis=1), qe[here, :], 1)
        near_largest = stats[0:1, here]
        largest = jnp.maximum(near_largest, jnp.max(scores, axis=0, keepdims=True))
        weights = jnp.exp2((scores - largest) * factor)
        shrink = jnp.exp2((near_largest - largest) * factor)
        inverse = 1.0 / (stats[1:2, here] * shrink + jnp.sum(weights, axis=0, keepdims=True))
        p_t[far, here] = (weights * inverse).astype(BF16)
        p_t[near, here] = (w_near[:, here] * (shrink * inverse)).astype(BF16)

    if n == 4:
        k_send(0).wait_recv()
        loop(steps, make_near)
        k_send(1).wait_recv()
        k_send(2).wait_recv()
        loop(steps, make_far)
    else:
        loop(n - 1, lambda k: k_send(k).wait_recv())
        loop(n - 1, lambda k: v_send(k).start())
        loop(steps, make_probs)
    g_copy.wait()

    def v_grads(k):
        send_buf[0, k] = dot(p_t[span(peer(k), rows), :], g_in[...]).astype(BF16)
        g_send(0, k).start()

    loop(n - 1, lambda k: v_grads(n - 2 - k))
    loop(n - 1, lambda k: v_send(k).wait_recv())

    def make_ds(at):
        here = span(at, chunk)
        dprobs = dot(vall[...], g_in[here, :], 1)
        p = p_t[:, here].astype(F32)
        delta = jnp.sum(p * dprobs, axis=0, keepdims=True)
        probs[:, here] = (p * (dprobs - delta)).astype(BF16)

    loop(steps, make_ds)

    def k_grads(k):
        send_buf[1, k] = (dot(probs[span(peer(k), rows), :], qe[:, :hd]) * scale).astype(BF16)
        g_send(1, k).start()

    loop(n - 1, lambda k: k_grads(n - 2 - k))
    own_dk = dot(probs[mine, :], qe[:, :hd]) * scale
    own_dv[...] = dot(p_t[mine, :], g_in[...])
    k_t[...] = kall[...].astype(F32).T.astype(BF16)
    v_t[...] = vall[...].astype(F32).T.astype(BF16)

    def make_o(at):
        here = span(at, chunk)
        o_ref[here, :] = dot(v_t[...], p_t[:, here]).T.astype(BF16)

    def make_dq(at):
        here = span(at, chunk)
        grad = dot(k_t[...], probs[:, here]).T * scale
        cosines, sines = spread(cos_ref, at, chunk, heads), spread(sin_ref, at, chunk, heads)
        dq_ref[here, :] = rotate(grad, cosines, -sines).astype(BF16)

    loop(steps, make_o)
    loop(steps, make_dq)

    def collect(kind, own):
        loop(n - 1, lambda k: g_send(kind, k).wait_recv())
        return own + jnp.sum(recv_buf[kind].astype(F32), axis=0)

    dv_ref[...] = collect(0, own_dv[...])
    dk_ref[...] = rotate(collect(1, own_dk), cos_ref[...], -sin_ref[...])

    def finish(k):
        k_send(k).wait_send()
        v_send(k).wait_send()
        g_send(0, k).wait_send()
        g_send(1, k).wait_send()

    loop(n - 1, finish)


def last_kernel(*refs):
    count = len(refs) // 2
    sem = refs[-1]
    copies = [pltpu.make_async_copy(refs[at], refs[count + at], sem.at[at]) for at in range(count)]
    for copy in copies:
        copy.start()
    for copy in copies:
        copy.wait()


def body(n, queries, key_heads, value_heads, out_grad, layout, documents):
    rows, heads, hd = queries.shape
    seq = layout.shape[0]
    flat = rows * heads
    small = seq <= 1024
    chunk = 256 if small else 128
    hbm = pl.BlockSpec(memory_space=pltpu.HBM)
    vmem = pl.BlockSpec(memory_space=pltpu.VMEM)
    shapes = (
        jax.ShapeDtypeStruct((flat, hd), BF16),
        jax.ShapeDtypeStruct((flat, hd), BF16),
        jax.ShapeDtypeStruct((rows, hd), F32),
        jax.ShapeDtypeStruct((rows, hd), F32),
    )
    carried = pl.pallas_call(
        functools.partial(main_kernel, n, heads, chunk),
        out_shape=shapes,
        in_specs=[hbm] * 7,
        out_specs=(vmem,) * 4,
        scratch_shapes=[
            pltpu.VMEM((seq, flat), BF16),
            pltpu.VMEM((hd, seq), BF16),
            pltpu.VMEM((rows, hd), F32),
            pltpu.VMEM((rows, hd), F32),
            pltpu.VMEM((2 * rows if n == 4 else 8, flat), F32),
            pltpu.VMEM((8, flat), F32),
            pltpu.SMEM((seq,), jnp.int32),
            pltpu.VMEM((1, seq), jnp.int32),
            pltpu.VMEM((1, seq), jnp.int32),
            pltpu.VMEM((rows, hd), BF16),
            pltpu.VMEM((flat, hd), BF16),
            pltpu.VMEM((flat, hd), BF16),
            pltpu.VMEM((flat, 2 * hd), BF16),
            pltpu.VMEM((seq, hd), BF16),
            pltpu.VMEM((seq, hd), BF16),
            pltpu.VMEM((hd, seq), BF16),
            pltpu.VMEM((seq, flat), BF16),
            pltpu.VMEM((seq, rows), BF16),
            pltpu.VMEM((2, n - 1, rows, hd), BF16),
            pltpu.VMEM((2, n - 1, rows, hd), BF16),
            pltpu.VMEM((rows, hd), F32),
            pltpu.SemaphoreType.DMA((7,)),
            pltpu.SemaphoreType.DMA((4, n - 1)),
            pltpu.SemaphoreType.DMA((4, n - 1)),
        ],
        compiler_params=pltpu.CompilerParams(
            collective_id=0, has_side_effects=True, vmem_limit_bytes=(40 if small else 58) * 1024 * 1024),
    )(*[pltpu.with_memory_space_constraint(operand, pltpu.HBM) for operand in (
        layout, layout.reshape(1, seq), documents.reshape(1, seq),
        queries.reshape(flat, hd), key_heads.reshape(rows, hd), value_heads.reshape(rows, hd),
        out_grad.reshape(flat, hd),
    )])
    out, dq, dk, dv = pl.pallas_call(
        last_kernel,
        out_shape=shapes,
        in_specs=[vmem] * 4,
        out_specs=(hbm,) * 4,
        scratch_shapes=[pltpu.SemaphoreType.DMA((4,))],
        compiler_params=pltpu.CompilerParams(vmem_limit_bytes=8 * 1024 * 1024),
    )(*carried)
    return (out.reshape(rows, heads, hd), dq.reshape(rows, heads, hd), dk, dv)


def solution(mesh):
    return jax.shard_map(
        functools.partial(body, mesh.shape["context"]),
        mesh=mesh,
        in_specs=(
            P(("dp", "context"), "tensor", None),
            P(("dp", "context"), "tensor", None),
            P(("dp", "context"), "tensor", None),
            P(("dp", "context"), "tensor", None),
            P("dp"),
            P("dp"),
        ),
        out_specs=(
            P(("dp", "context"), "tensor", None),
            P(("dp", "context"), "tensor", None),
            P(("dp", "context"), "tensor"),
            P(("dp", "context"), "tensor"),
        ),
        check_vma=False,
    )
```
